512 devices in a mesh: ctx: 16 (over y_hi, x), head: 32 (over z, y_lo, core).
Axes of the slice: x: 4, y: 8 (y_hi: 4, y_lo: 2; y = y_hi * 2 + y_lo), z: 8, core: 2. Of those that a mesh axis runs over, the one named last changes fastest.
Arguments:
- tokens: float32 [8192, 1024], P(('ctx', 'head')), may hold values from -60 to 60
- norm_gain: float32 [1024], replicated, may hold values from 0.1 to 1.9
- w_query: float32 [1024, 8192], P(None, 'head'), may hold values from -0.125 to 0.125
- w_key: float32 [1024, 8192], P(None, 'head'), may hold values from -6 to 6
- w_value: float32 [1024, 8192], P(None, 'head'), may hold values from -0.1875 to 0.1875
- w_out: float32 [8192, 1024], P('head'), may hold values from -0.0625 to 0.0625
- shift_heads: int32 [64], P('head'), may hold values from 0 to 1, as said below
- cotangent: float32 [8192, 1024], P(('ctx', 'head')), may hold values from -6 to 6
Outputs:
- mixed: float32 [8192, 1024], P(('ctx', 'head'))
- input_grad: float32 [8192, 1024], P(('ctx', 'head'))
The draws below stay inside these ranges and needn't reach their ends.
Inputs may be any that keep to these rules, and one draw needn't show every extreme that they name: For every i, exactly one of the heads 2i and 2i + 1 has shift_heads equal to 1.
All inputs are finite; a program needn't handle non-finite values.
Results may differ from the reference program's by a relative error of at most 0.0003.
Values sent between devices are 32-bit elements; how exact they have to be, the bound alone decides.
No kernel may reach another device: no remote copies, remote signals or barrier semaphores. Data moves between devices by JAX's collectives and lax.ppermute only.
A program may use at most 64 MiB of HBM per device.

```python
import math
import jax
import jax.numpy as jnp
from jax import lax

D = 1024
HD = 128
GROUP = 512
HEADS = 64
SHIFT = 256
TOKENS = 8192


def pair_weights(key):
    base = jnp.clip(jax.random.normal(jax.random.fold_in(key, 101), (D, HEADS * HD), jnp.float32), -6.0, 6.0) / math.sqrt(D)
    noise = jnp.clip(jax.random.normal(jax.random.fold_in(key, 102), (D, HEADS * HD), jnp.float32), -6.0, 6.0) / math.sqrt(D)
    return (base, noise)


def draw_w_query(key, part):
    base, noise = pair_weights(key)
    edge = 4.0 / math.sqrt(D)
    return jnp.clip(base, -edge, edge)


def draw_w_key(key, part):
    base, noise = pair_weights(key)
    return noise


def draw_tokens(key, part):
    return jnp.clip(jax.random.normal(jax.random.fold_in(key, 204), (TOKENS, D), jnp.float32), -6.0, 6.0)


def draw_shift_heads(key, part):
    picks = jax.random.randint(jax.random.fold_in(key, 301), (HEADS // 2,), 0, 2)
    return jnp.stack([picks, 1 - picks], axis=1).reshape(HEADS).astype(jnp.int32)


def level_of(rng, shape, pieces, smallest, top_value):
    level = 1.0
    for axis_at, shards_of in pieces:
        draws = jax.random.uniform(jax.random.fold_in(jax.random.fold_in(rng, 6), axis_at), (shards_of,), jnp.float32, smallest / len(pieces), top_value / len(pieces))
        level = level * jnp.repeat(jnp.exp(draws), shape[axis_at] // shards_of).reshape((-1,) + (1,) * (len(shape) - 1 - axis_at))
    return level


def bell_draw(own_key, extent, spread, most, pieces=(), kind=jnp.bfloat16):
    values = spread * jax.random.normal(own_key, extent, jnp.float32)
    if pieces:
        values = values * level_of(own_key, extent, pieces, -0.22, 0.18)
    return jnp.clip(values, -most, most).astype(kind)


def setup_inputs(seed: int = 0) -> dict:
    key_of = jax.random.split(jax.random.key(seed), 9)
    tokens = draw_tokens(jax.random.fold_in(key_of[8], 71), 0)
    norm_gain = jnp.clip(1.0 + 0.18 * jax.random.normal(key_of[1], (D,), jnp.float32), 0.1, 1.9)
    w_query = draw_w_query(jax.random.fold_in(key_of[8], 71), 0)
    w_key = draw_w_key(jax.random.fold_in(key_of[8], 71), 0)
    w_value = bell_draw(key_of[4], (D, HEADS * HD), D ** -0.5, 0.1875, ((1, 32),), jnp.float32)
    w_out = bell_draw(key_of[5], (HEADS * HD, D), (HEADS * HD) ** -0.5, 0.0625, ((0, 32),), jnp.float32)
    shift_heads = draw_shift_heads(jax.random.fold_in(key_of[8], 71), 0)
    cotangent = bell_draw(key_of[7], (TOKENS, D), 1.0, 6.0, ((0, 512),), jnp.float32)
    return dict(tokens=tokens, norm_gain=norm_gain, w_query=w_query, w_key=w_key, w_value=w_value, w_out=w_out, shift_heads=shift_heads, cotangent=cotangent)


precise = lax.Precision.HIGHEST

def rms_rows(values, gain):
    return values * lax.rsqrt(lax.optimization_barrier(jnp.mean(values * values, axis=-1, keepdims=True)) + 1e-06) * gain

def head_attention(packed):
    query, keys, values, moved = packed
    length = query.shape[0]
    offset = (moved * SHIFT).astype(jnp.int32)
    order = ((jnp.arange(length, dtype=jnp.int32) + offset) % length).astype(jnp.int32)
    query_rows = jnp.take(query, order, axis=0).reshape(length // GROUP, GROUP, -1)
    key_rows = jnp.take(keys, order, axis=0).reshape(length // GROUP, GROUP, -1)
    value_rows = jnp.take(values, order, axis=0).reshape(length // GROUP, GROUP, -1)
    scores = jnp.einsum('gqd,gkd->gqk', query_rows, key_rows, precision=precise) * (1.0 / math.sqrt(HD))
    row_max = lax.stop_gradient(lax.optimization_barrier(jnp.max(scores, axis=-1, keepdims=True)))
    powers = jnp.exp(scores - row_max)
    probs = powers / lax.optimization_barrier(jnp.sum(powers, axis=-1, keepdims=True))
    result = jnp.einsum('gqk,gkd->gqd', probs, value_rows, precision=precise).reshape(length, -1)
    back = ((jnp.arange(length, dtype=jnp.int32) - offset) % length).astype(jnp.int32)
    return jnp.take(result, back, axis=0)

def reference(tokens, norm_gain, w_query, w_key, w_value, w_out, shift_heads, cotangent):

    def forward(token_rows):
        length = token_rows.shape[0]
        normed = rms_rows(token_rows, norm_gain)

        def project(weight):
            return jnp.dot(normed, weight, precision=precise).reshape(length, HEADS, HD).transpose(1, 0, 2)
        heads_out = lax.map(head_attention, (project(w_query), project(w_key), project(w_value), shift_heads))
        attention = heads_out.transpose(1, 0, 2).reshape(length, HEADS * HD)
        return token_rows + jnp.dot(attention, w_out, precision=precise)
    mixed, pullback = jax.vjp(forward, tokens)
    input_grad = pullback(cotangent)[0]
    return (mixed, input_grad)
```

```python
import math

import jax
import jax.numpy as jnp
from jax import lax
from jax.sharding import PartitionSpec as P

precise = lax.Precision.HIGHEST
steady = lax.Precision.HIGH
CHIP = 2


def core_swap(x):
    length = lax.axis_size("head")
    return lax.ppermute(x, "head", [(i, i ^ 1) for i in range(length)])


def same_core():
    length = lax.axis_size("head")
    return [list(range(core, length, CHIP)) for core in range(CHIP)]


def gather_chips(rows):
    groups = same_core()
    sent = jnp.broadcast_to(rows[None], (len(groups[0]),) + rows.shape)
    return lax.all_to_all(sent, "head", 0, 0, tiled=True, axis_index_groups=groups)


def gather_cores(own):
    other = core_swap(own)
    core = lax.axis_index("head") % CHIP
    first = jnp.where(core == 0, own, other)
    last = jnp.where(core == 0, other, own)
    return jnp.stack([first, last], axis=1).reshape(-1, own.shape[2])


def chip_terms(terms):
    length = lax.axis_size("head")
    core = lax.axis_index("head") % CHIP
    split = terms.reshape(length // CHIP, CHIP, -1, terms.shape[1])
    kept = jnp.where(core == 0, split[:, 0], split[:, 1])
    given = jnp.where(core == 0, split[:, 1], split[:, 0])
    return kept + core_swap(given)


def sum_chips(part):
    swapped = lax.all_to_all(part, "head", 0, 0, tiled=True, axis_index_groups=same_core())
    return jnp.sum(swapped, axis=0)


def padded(block, sides, width):
    for axis, dim in sides:
        count = lax.axis_size(axis)
        forward = [(i, i + 1) for i in range(count - 1)]
        forward.append((count - 1, 0))
        backward = [(target, source) for source, target in forward]
        low = lax.ppermute(
            lax.slice_in_dim(block, block.shape[dim] - width, None, axis=dim), axis, forward
        )
        high = lax.ppermute(lax.slice_in_dim(block, 0, width, axis=dim), axis, backward)
        block = jnp.concatenate([low, block, high], axis=dim)
    return block


def from_behind(x, axis, by):
    length = lax.axis_size(axis)
    return lax.ppermute(x, axis, [(i, (i + by) % length) for i in range(length)])


def rms_rows(values, gain):
    return values * lax.rsqrt(jnp.mean(values * values, axis=-1, keepdims=True) + 1e-06) * gain


def softmax_last(scores):
    row_max = jnp.max(scores, axis=-1, keepdims=True)
    powers = jnp.exp(scores - row_max)
    return powers / jnp.sum(powers, axis=-1, keepdims=True)


def attend(query, keys, values, score_scale):
    probs = softmax_last(jnp.einsum("gqd,gkd->gqk", query, keys, precision=precise) * score_scale)
    return (probs, jnp.einsum("gqk,gkd->gqd", probs, values, precision=precise))


def attend_back(query, keys, values, probs, output, grad_out, score_scale):
    grad_values = jnp.einsum("gqk,gqd->gkd", probs, grad_out, precision=precise)
    grad_probs = jnp.einsum("gqd,gkd->gqk", grad_out, values, precision=precise)
    inner = jnp.sum(grad_out * output, axis=-1, keepdims=True)
    grad_scores = probs * (grad_probs - inner) * score_scale
    grad_query = jnp.einsum("gqk,gkd->gqd", grad_scores, keys, precision=precise)
    grad_keys = jnp.einsum("gqk,gqd->gkd", grad_scores, query, precision=precise)
    return (grad_query, grad_keys, grad_values)


def local(tokens, norm_gain, w_query, w_key, w_value, w_out, shift_heads, cotangent):
    own = gather_chips(tokens)
    own, cot_later = lax.optimization_barrier((own, cotangent))
    cot_own = gather_chips(cot_later)
    gathered = gather_cores(own)
    group_len = gathered.shape[0]
    half_len = group_len // 2
    width = w_query.shape[1]
    head_dim = width // 2
    score_scale = 1.0 / math.sqrt(head_dim)
    normed = rms_rows(gathered, norm_gain)
    query = jnp.dot(normed, w_query, precision=precise)
    keys = jnp.dot(normed, w_key, precision=precise)
    values = jnp.dot(normed, w_value, precision=steady)
    second = shift_heads[1] == 1

    def split_heads(matrix):
        paired = matrix.reshape(group_len, 2, head_dim)
        moved = jnp.where(second, paired[:, 1], paired[:, 0])
        still = jnp.where(second, paired[:, 0], paired[:, 1])
        return (moved, still)

    def join_heads(moved, still):
        first_head = jnp.where(second, still, moved)
        second_head = jnp.where(second, moved, still)
        return jnp.stack([first_head, second_head], axis=1).reshape(group_len, width)

    query_moved, query_still = split_heads(query)
    keys_moved, keys_still = split_heads(keys)
    values_moved, values_still = split_heads(values)
    probs_still, out_still = attend(
        query_still[None], keys_still[None], values_still[None], score_scale
    )
    rim = padded(jnp.concatenate([keys_moved, values_moved], axis=1), (("ctx", 0),), half_len)
    keys_rim = rim[:, :head_dim].reshape(2, group_len, head_dim)
    values_rim = rim[:, head_dim : 2 * head_dim].reshape(2, group_len, head_dim)
    query_halves = query_moved.reshape(2, half_len, head_dim)
    probs_moved, out_moved = attend(query_halves, keys_rim, values_rim, score_scale)
    attention = join_heads(out_moved.reshape(group_len, head_dim), out_still[0])
    out_terms = jnp.dot(attention, w_out, precision=steady)
    out_part = chip_terms(out_terms)
    cot_own, out_part = lax.optimization_barrier((cot_own, out_part))
    out_sum = sum_chips(out_part)
    cot_rows = gather_cores(cot_own)
    grad_attention = jnp.dot(cot_rows, w_out.T, precision=steady)
    grad_moved, grad_still = split_heads(grad_attention)
    grad_query_still, grad_keys_still, grad_values_still = attend_back(
        query_still[None],
        keys_still[None],
        values_still[None],
        probs_still,
        out_still,
        grad_still[None],
        score_scale,
    )
    grad_query_halves, grad_keys_rim, grad_values_rim = attend_back(
        query_halves,
        keys_rim,
        values_rim,
        probs_moved,
        out_moved,
        grad_moved.reshape(2, half_len, head_dim),
        score_scale,
    )
    grad_query_moved = grad_query_halves.reshape(group_len, head_dim)
    rim_grads = jnp.concatenate(
        [
            grad_keys_rim.reshape(2 * group_len, head_dim),
            grad_values_rim.reshape(2 * group_len, head_dim),
        ],
        axis=1,
    )
    from_right = from_behind(rim_grads[:half_len], "ctx", -1)
    from_left = from_behind(rim_grads[group_len + half_len :], "ctx", 1)
    own_rows = rim_grads[half_len : half_len + group_len] + jnp.concatenate(
        [from_left, from_right], axis=0
    )
    grad_keys_moved = own_rows[:, :head_dim]
    grad_values_moved = own_rows[:, head_dim:]
    grad_terms = jnp.dot(
        join_heads(grad_query_moved, grad_query_still[0]), w_query.T, precision=steady
    )
    grad_terms = grad_terms + jnp.dot(
        join_heads(grad_keys_moved, grad_keys_still[0]), w_key.T, precision=steady
    )
    grad_terms = grad_terms + jnp.dot(
        join_heads(grad_values_moved, grad_values_still[0]), w_value.T, precision=steady
    )
    grad_sum = sum_chips(chip_terms(grad_terms))
    mixed = tokens + out_sum
    inverse = lax.rsqrt(jnp.mean(tokens * tokens, axis=-1, keepdims=True) + 1e-06)
    weighted = grad_sum * norm_gain
    correction = jnp.mean(weighted * tokens, axis=-1, keepdims=True)
    input_grad = (
        cotangent + weighted * inverse - tokens * (inverse * inverse * inverse) * correction
    )
    return (mixed, input_grad)


def solution(mesh):
    placed = (
        P(("ctx", "head"), None),
        P(),
        P(None, "head"),
        P(None, "head"),
        P(None, "head"),
        P("head", None),
        P("head"),
        P(("ctx", "head"), None),
    )
    return jax.shard_map(
        local,
        mesh=mesh,
        in_specs=placed,
        out_specs=(P(("ctx", "head"), None), P(("ctx", "head"), None)),
        check_vma=False,
    )
```

```python
import functools
import math

import jax
import jax.numpy as jnp
from jax import lax
from jax.experimental import pallas as pl
from jax.experimental.pallas import tpu as pltpu
from jax.sharding import PartitionSpec as P

F32, BF16 = jnp.float32, jnp.bfloat16
NN, NT, TN = ((1,), (0,)), ((1,), (1,)), ((0,), (0,))


def parts2(x):
    high = x.astype(BF16)
    return high, (x - high.astype(F32)).astype(BF16)


def parts3(x):
    high = x.astype(BF16)
    rest = x - high.astype(F32)
    middle = rest.astype(BF16)
    return high, middle, (rest - middle.astype(F32)).astype(BF16)


def mul(a, b, dims):
    return lax.dot_general(a, b, (dims, ((), ())), preferred_element_type=F32)


def mul3(a, b, dims):
    return mul(a[0], b[0], dims) + (mul(a[0], b[1], dims) + mul(a[1], b[0], dims))


def mul6(a, b, dims):
    small = mul(a[1], b[1], dims) + mul(a[0], b[2], dims) + mul(a[2], b[0], dims)
    return mul(a[0], b[0], dims) + (mul(a[0], b[1], dims) + mul(a[1], b[0], dims) + small)


def cat(a, b):
    return jnp.concatenate([a, b], axis=1)


def scores6(a, b):
    (ah, am, al), (bh, bm, bl) = a, b
    wide = cat(bh, bm)
    return mul(cat(ah, ah), wide, NT) + (mul(cat(am, am), wide, NT) + mul(cat(ah, al), cat(bl, bh), NT))


def scores3(a, b):
    (ah, am), (bh, bm) = a, b
    return mul(cat(ah, am), cat(bh, bh), NT) + mul(ah, bm, NT)


def weigh3(a, b, dims):
    width = b[0].shape[1]
    both = mul(a[0], cat(b[0], b[1]), dims)
    return both[:, :width] + (both[:, width:] + mul(a[1], b[0], dims))


def head_cols(flag_ref, width):
    second = flag_ref[0]
    moved = pl.multiple_of(second * width, width)
    still = pl.multiple_of((1 - second) * width, width)
    return pl.ds(moved, width), pl.ds(still, width)


def normed_parts(own_ref, other_ref, gain_ref, refs):
    rows = own_ref.shape[1]
    for slot, source in enumerate((own_ref, other_ref)):

        @pl.loop(0, 2)
        def _(half):
            x = source[half]
            x = x * lax.rsqrt(jnp.mean(x * x, axis=-1, keepdims=True) + 1e-06) * gain_ref[...]
            at = pl.ds(pl.multiple_of((2 * half + slot) * rows, rows), rows)
            for ref, part in zip(refs, parts3(x)):
                ref[at] = part


def softmax_rows(scores):
    powers = jnp.exp(scores - jnp.max(scores, axis=-1, keepdims=True))
    return powers / jnp.sum(powers, axis=-1, keepdims=True)


def rim_kernel(flag_ref, own_ref, other_ref, gain_ref, wk_ref, wv_ref, first_ref, last_ref, nh, nm, nl):
    normed_parts(own_ref, other_ref, gain_ref, (nh, nm, nl))
    moved, _ = head_cols(flag_ref, wk_ref.shape[1] // 2)
    half = first_ref.shape[0]
    both = mul6((nh[...], nm[...], nl[...]), parts3(cat(wk_ref[:, moved], wv_ref[:, moved])), NN)
    first_ref[...] = both[:half]
    last_ref[...] = both[half:]


def still_kernel(scale, flag_ref, own_ref, other_ref, gain_ref, wq_ref, wk_ref, wv_ref, q_ref, kv_ref, ps_ref, os_ref, nh, nm, nl):
    normed_parts(own_ref, other_ref, gain_ref, (nh, nm, nl))
    hd = wk_ref.shape[1] // 2
    _, still = head_cols(flag_ref, hd)
    n = (nh[...], nm[...], nl[...])
    q_ref[...] = mul6(n, parts3(wq_ref[...]), NN)
    kv_ref[...] = mul6(n, parts3(cat(wk_ref[:, still], wv_ref[:, still])), NN)
    scores = scores6(parts3(q_ref[:, still]), parts3(kv_ref[:, :hd])) * scale
    probs = softmax_rows(scores)
    ps_ref[...] = probs
    os_ref[...] = weigh3(parts2(probs), parts2(kv_ref[:, hd:]), NN)


def moved_kernel(scale, flag_ref, q_ref, first_ref, last_ref, low_ref, high_ref, os_ref, wo_ref, pm_ref, mine_ref, theirs_ref, both):
    hd = os_ref.shape[1]
    half = first_ref.shape[0]
    moved, still = head_cols(flag_ref, hd)
    for g, (a_ref, b_ref) in enumerate(((low_ref, first_ref), (last_ref, high_ref))):
        rim = jnp.concatenate([a_ref[...], b_ref[...]], axis=0)
        at = pl.ds(g * half, half)
        scores = scores6(parts3(q_ref[at, moved]), parts3(rim[:, :hd])) * scale
        probs = softmax_rows(scores)
        pm_ref[g] = probs
        both[at, moved] = weigh3(parts2(probs), parts2(rim[:, hd:]), NN)
    both[:, still] = os_ref[...]
    rows = mine_ref.shape[1]
    out = mul3(parts2(both[...]), parts2(wo_ref[...]), NN)
    for g in range(2):
        mine_ref[g] = out[2 * g * rows : (2 * g + 1) * rows]
        theirs_ref[g] = out[(2 * g + 1) * rows : (2 * g + 2) * rows]


def group_back(query, kv, probs, grad_out, scale):
    hd = query.shape[1]
    q, k, v, g = parts2(query), parts2(kv[:, :hd]), parts2(kv[:, hd:]), parts2(grad_out)
    grad_probs = scores3(g, v)
    inner = jnp.sum(probs * grad_probs, axis=-1, keepdims=True)
    grad_values = weigh3(parts2(probs), g, TN)
    grad_scores = parts2(probs * (grad_probs - inner) * scale)
    grad_query = weigh3(grad_scores, k, NN)
    grad_keys = weigh3(grad_scores, q, TN)
    return grad_query, cat(grad_keys, grad_values)


def moved_back_kernel(scale, flag_ref, own_ref, other_ref, wo_ref, q_ref, first_ref, last_ref, low_ref, high_ref, pm_ref, ga_ref, dq_ref, left_ref, right_ref, keep_ref, ch, cm):
    hd = q_ref.shape[1] // 2
    half = first_ref.shape[0]
    rows = own_ref.shape[1]
    moved, _ = head_cols(flag_ref, hd)
    for slot, source in enumerate((own_ref, other_ref)):
        for g in range(2):
            at = pl.ds((2 * g + slot) * rows, rows)
            ch[at], cm[at] = parts2(source[g])
    ga_ref[...] = mul3((ch[...], cm[...]), parts2(wo_ref[...]), NT)
    for g, (a_ref, b_ref) in enumerate(((low_ref, first_ref), (last_ref, high_ref))):
        rim = jnp.concatenate([a_ref[...], b_ref[...]], axis=0)
        at = pl.ds(g * half, half)
        gq, gkv = group_back(q_ref[at, moved], rim, pm_ref[g], ga_ref[at, moved], scale)
        dq_ref[at] = gq
        if g == 0:
            left_ref[...] = gkv[:half]
            keep_ref[:half] = gkv[half:]
        else:
            keep_ref[half:] = gkv[:half]
            right_ref[...] = gkv[half:]


def still_back_kernel(scale, flag_ref, ga_ref, q_ref, kv_ref, ps_ref, dqm_ref, wq_ref, wk_ref, wv_ref, terms_ref, both):
    hd = dqm_ref.shape[1]
    moved, still = head_cols(flag_ref, hd)
    gq, gkv = group_back(q_ref[:, still], kv_ref[...], ps_ref[...], ga_ref[:, still], scale)
    both[:, moved] = dqm_ref[...]
    both[:, still] = gq
    terms_ref[...] = mul3(parts2(both[...]), parts2(wq_ref[...]), NT) + mul3(parts2(gkv), parts2(cat(wk_ref[:, still], wv_ref[:, still])), NT)


def finish_kernel(flag_ref, terms_ref, keep_ref, left_ref, right_ref, wk_ref, wv_ref, mine_ref, theirs_ref):
    moved, _ = head_cols(flag_ref, wk_ref.shape[1] // 2)
    rows = mine_ref.shape[1]
    grads = keep_ref[...] + jnp.concatenate([left_ref[...], right_ref[...]], axis=0)
    out = terms_ref[...] + mul3(parts2(grads), parts2(cat(wk_ref[:, moved], wv_ref[:, moved])), NT)
    for h in range(2):
        mine_ref[h] = out[2 * h * rows : (2 * h + 1) * rows]
        theirs_ref[h] = out[(2 * h + 1) * rows : (2 * h + 2) * rows]


def call(kernel, name, shapes, flag, *operands, scratch=(), flops=0):
    vmem = pl.BlockSpec(memory_space=pltpu.VMEM)
    out = [jax.ShapeDtypeStruct(s, F32) for s in shapes]
    size = sum(4 * math.prod(s) for s in shapes) + sum(4 * x.size for x in operands)
    return pl.pallas_call(
        kernel,
        out_shape=out,
        in_specs=[pl.BlockSpec(memory_space=pltpu.SMEM)] + [vmem] * len(operands),
        out_specs=[vmem] * len(shapes),
        scratch_shapes=list(scratch),
        compiler_params=pltpu.CompilerParams(vmem_limit_bytes=LIMIT),
        cost_estimate=pl.CostEstimate(flops=int(flops), bytes_accessed=size, transcendentals=0),
        name=name,
    )(flag, *operands)


LIMIT = 30 << 20


def rim_call(flag, own, other, gain, wk, wv):
    D, W = wk.shape
    T = 4 * own.shape[1]
    return call(rim_kernel, "rim_forward", [(T // 2, W)] * 2, flag, own, other, gain, wk, wv,
                scratch=[pltpu.VMEM((T, D), BF16)] * 3, flops=2 * T * D * W * 6)


def still_call(scale, flag, own, other, gain, wq, wk, wv):
    D, W = wk.shape
    T = 4 * own.shape[1]
    hd = W // 2
    return call(functools.partial(still_kernel, scale), "still_forward", [(T, W)] * 2 + [(T, T), (T, hd)], flag, own, other, gain, wq, wk, wv,
                scratch=[pltpu.VMEM((T, D), BF16)] * 3, flops=2 * T * D * hd * 24 + 2 * T * T * hd * 9)


def moved_call(scale, flag, q, first, last, low, high, out_still, wo):
    T, hd = out_still.shape
    D = wo.shape[1]
    return call(functools.partial(moved_kernel, scale), "moved_forward", [(2, T // 2, T), (2, T // 4, D), (2, T // 4, D)],
                flag, q, first, last, low, high, out_still, wo, scratch=[pltpu.VMEM((T, 2 * hd), F32)], flops=2 * T * D * hd * 6 + 2 * T * T * hd * 9)


def moved_back_call(scale, flag, own, other, wo, q, first, last, low, high, pm):
    T, hd = q.shape[0], q.shape[1] // 2
    D = wo.shape[1]
    return call(functools.partial(moved_back_kernel, scale), "moved_backward",
                [(T, 2 * hd), (T, hd), (T // 2, 2 * hd), (T // 2, 2 * hd), (T, 2 * hd)],
                flag, own, other, wo, q, first, last, low, high, pm,
                scratch=[pltpu.VMEM((T, D), BF16)] * 2, flops=2 * T * D * hd * 6 + 2 * T * T * hd * 12)


def still_back_call(scale, flag, ga, q, kv, ps, dqm, wq, wk, wv):
    T, hd = dqm.shape
    D = wq.shape[0]
    return call(functools.partial(still_back_kernel, scale), "still_backward", [(T, D)], flag, ga, q, kv, ps, dqm, wq, wk, wv,
                scratch=[pltpu.VMEM((T, 2 * hd), F32)], flops=2 * T * D * hd * 12 + 2 * T * T * hd * 12)[0]


def finish_call(flag, terms, keep, left, right, wk, wv):
    T, D = terms.shape
    return call(finish_kernel, "finish", [(2, T // 4, D)] * 2, flag, terms, keep, left, right, wk, wv, flops=2 * T * D * wk.shape[1] * 3)


CHIP = 2


def core_swap(x):
    length = lax.axis_size("head")
    return lax.ppermute(x, "head", [(i, i ^ 1) for i in range(length)])


def same_core():
    length = lax.axis_size("head")
    return [list(range(core, length, CHIP)) for core in range(CHIP)]


def gather_chips(rows):
    groups = same_core()
    chips = len(groups[0])
    sent = jnp.broadcast_to(rows[None], (chips,) + rows.shape)
    own = lax.all_to_all(sent, "head", 0, 0, tiled=True, axis_index_groups=groups)
    return own.reshape(2, -1, rows.shape[1])


def sum_chips(part):
    groups = same_core()
    chips = len(groups[0])
    split = part.reshape(chips, -1, part.shape[2])
    swapped = lax.all_to_all(split, "head", 0, 0, tiled=True, axis_index_groups=groups)
    return jnp.sum(swapped, axis=0)


def along(x, by):
    length = lax.axis_size("ctx")
    return lax.ppermute(x, "ctx", [(i, (i + by) % length) for i in range(length)])


def local(tokens, norm_gain, w_query, w_key, w_value, w_out, shift_heads, cotangent):
    scale = 1.0 / math.sqrt(w_query.shape[1] // 2)
    flag = shift_heads[1:2]
    gain = norm_gain[None]
    own = gather_chips(tokens)
    own, cot_later = lax.optimization_barrier((own, cotangent))
    other = core_swap(own)
    cot_own = gather_chips(cot_later)
    first, last = rim_call(flag, own, other, gain, w_key, w_value)
    low, high = along(last, 1), along(first, -1)
    query, kv_still, probs_still, out_still = still_call(scale, flag, own, other, gain, w_query, w_key, w_value)
    probs_moved, mine, theirs = moved_call(scale, flag, query, first, last, low, high, out_still, w_out)
    out_part = mine + core_swap(theirs)
    cot_own, out_part = lax.optimization_barrier((cot_own, out_part))
    out_sum = sum_chips(out_part)
    cot_other = core_swap(cot_own)
    grad_attention, grad_query, left, right, keep = moved_back_call(
        scale, flag, cot_own, cot_other, w_out, query, first, last, low, high, probs_moved
    )
    from_left, from_right = along(right, 1), along(left, -1)
    terms = still_back_call(
        scale, flag, grad_attention, query, kv_still, probs_still, grad_query, w_query, w_key, w_value
    )
    mine, theirs = finish_call(flag, terms, keep, from_left, from_right, w_key, w_value)
    grad_sum = sum_chips(mine + core_swap(theirs))
    mixed = tokens + out_sum
    inverse = lax.rsqrt(jnp.mean(tokens * tokens, axis=-1, keepdims=True) + 1e-06)
    weighted = grad_sum * norm_gain
    correction = jnp.mean(weighted * tokens, axis=-1, keepdims=True)
    input_grad = (
        cotangent + weighted * inverse - tokens * (inverse * inverse * inverse) * correction
    )
    return (mixed, input_grad)


def solution(mesh):
    placed = (
        P(("ctx", "head"), None),
        P(),
        P(None, "head"),
        P(None, "head"),
        P(None, "head"),
        P("head", None),
        P("head"),
        P(("ctx", "head"), None),
    )
    return jax.shard_map(
        local,
        mesh=mesh,
        in_specs=placed,
        out_specs=(P(("ctx", "head"), None), P(("ctx", "head"), None)),
        check_vma=False,
    )
```

```python
import functools
import math

import jax
import jax.numpy as jnp
from jax import lax
from jax.experimental import pallas as pl
from jax.experimental.pallas import tpu as pltpu
from jax.sharding import PartitionSpec as P

F32, BF16 = jnp.float32, jnp.bfloat16
NN, NT, TN = ((1,), (0,)), ((1,), (1,)), ((0,), (0,))


def parts2(x):
    high = x.astype(BF16)
    return high, (x - high.astype(F32)).astype(BF16)


def parts3(x):
    high = x.astype(BF16)
    rest = x - high.astype(F32)
    middle = rest.astype(BF16)
    return high, middle, (rest - middle.astype(F32)).astype(BF16)


def mul(a, b, dims):
    return lax.dot_general(a, b, (dims, ((), ())), preferred_element_type=F32)


def mul3(a, b, dims):
    return mul(a[0], b[0], dims) + (mul(a[0], b[1], dims) + mul(a[1], b[0], dims))


def mul6(a, b, dims):
    small = mul(a[1], b[1], dims) + mul(a[0], b[2], dims) + mul(a[2], b[0], dims)
    return mul(a[0], b[0], dims) + (mul(a[0], b[1], dims) + mul(a[1], b[0], dims) + small)


def cat(a, b):
    return jnp.concatenate([a, b], axis=1)


def scores6(a, b):
    (ah, am, al), (bh, bm, bl) = a, b
    wide = cat(bh, bm)
    return mul(cat(ah, ah), wide, NT) + (mul(cat(am, am), wide, NT) + mul(cat(ah, al), cat(bl, bh), NT))


def scores3(a, b):
    (ah, am), (bh, bm) = a, b
    return mul(cat(ah, am), cat(bh, bh), NT) + mul(ah, bm, NT)


def weigh3(a, b, dims):
    width = b[0].shape[1]
    both = mul(a[0], cat(b[0], b[1]), dims)
    return both[:, :width] + (both[:, width:] + mul(a[1], b[0], dims))


def head_cols(flag_ref, width):
    second = flag_ref[0]
    moved = pl.multiple_of(second * width, width)
    still = pl.multiple_of((1 - second) * width, width)
    return pl.ds(moved, width), pl.ds(still, width)


def normed_parts(own, other, gain_ref, refs):
    for slot, source in enumerate((own, other)):
        rows = source.shape[1]

        @pl.loop(0, 2)
        def _(half):
            x = source[half]
            x = x * lax.rsqrt(jnp.mean(x * x, axis=-1, keepdims=True) + 1e-06) * gain_ref[...]
            at = pl.ds(pl.multiple_of((2 * half + slot) * rows, rows), rows)
            for ref, part in zip(refs, parts3(x)):
                ref[at] = part


def softmax_rows(scores):
    powers = jnp.exp(scores - jnp.max(scores, axis=-1, keepdims=True))
    return powers / jnp.sum(powers, axis=-1, keepdims=True)


def rim_kernel(flag_ref, own, wk, wv, other, gain_ref, first_ref, last_ref, nh, nm, nl):
    normed_parts(own, other, gain_ref, (nh, nm, nl))
    moved, _ = head_cols(flag_ref, wk.shape[1] // 2)
    half = first_ref.shape[0]
    both = mul6((nh[...], nm[...], nl[...]), parts3(cat(wk[:, moved], wv[:, moved])), NN)
    first_ref[...] = both[:half]
    last_ref[...] = both[half:]


def still_kernel(scale, flag_ref, wk, wv, wq, nh, nm, nl, qm_ref, qs_ref, kv_ref, ps_ref, os_ref, q_ref):
    hd = wk.shape[1] // 2
    moved, still = head_cols(flag_ref, hd)
    n = (nh[...], nm[...], nl[...])
    kv_ref[...] = mul6(n, parts3(cat(wk[:, still], wv[:, still])), NN)
    q_ref[...] = mul6(n, parts3(wq[...]), NN)
    qm_ref[...] = q_ref[:, moved]
    qs_ref[...] = q_ref[:, still]
    scores = scores6(parts3(qs_ref[...]), parts3(kv_ref[:, :hd])) * scale
    probs = softmax_rows(scores)
    ps_ref[...] = probs
    os_ref[...] = weigh3(parts2(probs), parts2(kv_ref[:, hd:]), NN)


def moved_kernel(scale, flag_ref, q_ref, first_ref, last_ref, wo, os_ref, low_ref, high_ref, pm_ref, mine_ref, theirs_ref, both):
    hd = os_ref.shape[1]
    half = first_ref.shape[0]
    moved, still = head_cols(flag_ref, hd)
    for g, (a_ref, b_ref) in enumerate(((low_ref, first_ref), (last_ref, high_ref))):
        rim = jnp.concatenate([a_ref[...], b_ref[...]], axis=0)
        at = pl.ds(g * half, half)
        scores = scores6(parts3(q_ref[at]), parts3(rim[:, :hd])) * scale
        probs = softmax_rows(scores)
        pm_ref[g] = probs
        both[at, moved] = weigh3(parts2(probs), parts2(rim[:, hd:]), NN)
    both[:, still] = os_ref[...]
    rows = mine_ref.shape[1]
    out = mul3(parts2(both[...]), parts2(wo[...]), NN)
    for g in range(2):
        mine_ref[g] = out[2 * g * rows : (2 * g + 1) * rows]
        theirs_ref[g] = out[(2 * g + 1) * rows : (2 * g + 2) * rows]


def group_back(query, kv, probs, grad_out, scale):
    hd = query.shape[1]
    q, k, v, g = parts2(query), parts2(kv[:, :hd]), parts2(kv[:, hd:]), parts2(grad_out)
    grad_probs = scores3(g, v)
    inner = jnp.sum(probs * grad_probs, axis=-1, keepdims=True)
    grad_values = weigh3(parts2(probs), g, TN)
    grad_scores = parts2(probs * (grad_probs - inner) * scale)
    grad_query = weigh3(grad_scores, k, NN)
    grad_keys = weigh3(grad_scores, q, TN)
    return grad_query, cat(grad_keys, grad_values)


def moved_back_kernel(scale, flag_ref, q, rim_low, rim_first, pm, rim_last, rim_high, own, other, wo, gs_ref, dq_ref, left_ref, right_ref, keep_ref, ch, cm, ga_ref):
    for slot, source in enumerate((own, other)):
        rows = source.shape[1]
        for g in range(2):
            at = pl.ds((2 * g + slot) * rows, rows)
            ch[at], cm[at] = parts2(source[g])
    moved, still = head_cols(flag_ref, q.shape[1])
    ga_ref[...] = mul3((ch[...], cm[...]), parts2(wo[...]), NT)
    gs_ref[...] = ga_ref[:, still]
    for g, (a, b) in enumerate(((rim_low, rim_first), (rim_last, rim_high))):
        rim = jnp.concatenate([a[...], b[...]], axis=0)
        half = left_ref.shape[0]
        at = pl.ds(g * half, half)
        gq, gkv = group_back(q[at], rim, pm[g], ga_ref[at, moved], scale)
        dq_ref[at] = gq
        if g == 0:
            left_ref[...] = gkv[:half]
            keep_ref[:half] = gkv[half:]
        else:
            keep_ref[half:] = gkv[:half]
            right_ref[...] = gkv[half:]


def still_back_kernel(scale, flag_ref, ga, kv, ps, q, dqm, wq, wk, wv, terms_ref, both):
    hd = dqm.shape[1]
    moved, still = head_cols(flag_ref, hd)
    gq, gkv = group_back(q[...], kv[...], ps[...], ga[...], scale)
    both[:, moved] = dqm[...]
    both[:, still] = gq
    terms_ref[...] = mul3(parts2(both[...]), parts2(wq[...]), NT)
    terms_ref[...] += mul3(parts2(gkv), parts2(cat(wk[:, still], wv[:, still])), NT)


def finish_kernel(flag_ref, wk, wv, terms_ref, keep_ref, left_ref, right_ref, mine_ref, theirs_ref):
    moved, _ = head_cols(flag_ref, wk.shape[1] // 2)
    rows = mine_ref.shape[1]
    grads = keep_ref[...] + jnp.concatenate([left_ref[...], right_ref[...]], axis=0)
    out = terms_ref[...] + mul3(parts2(grads), parts2(cat(wk[:, moved], wv[:, moved])), NT)
    for h in range(2):
        mine_ref[h] = out[2 * h * rows : (2 * h + 1) * rows]
        theirs_ref[h] = out[(2 * h + 1) * rows : (2 * h + 2) * rows]


class Fetched:
    def __init__(self, source, held, semaphore):
        self.copy, self.held, self.waiting = pltpu.make_async_copy(source, held, semaphore), held, True
        self.copy.start()

    @property
    def shape(self):
        return self.held.shape

    def __getitem__(self, at):
        if self.waiting:
            self.copy.wait()
            self.waiting = False
        return self.held[at]


def call(kernel, shapes, flag, operands, scratch=(), flops=0, fetched=0, away_out=False):
    vmem = pl.BlockSpec(memory_space=pltpu.VMEM)
    out = [s if isinstance(s, jax.ShapeDtypeStruct) else jax.ShapeDtypeStruct(s, F32) for s in shapes]
    away = operands[:fetched]

    def body(flag_ref, *refs):
        if away:
            sources, rest, held, semaphores = refs[:fetched], refs[fetched : -1 - fetched], refs[-1 - fetched : -1], refs[-1]
            refs = [Fetched(x, h, semaphores.at[i]) for i, (x, h) in enumerate(zip(sources, held))] + list(rest)
        kernel(flag_ref, *refs)

    return pl.pallas_call(
        body,
        out_shape=[pltpu.HBM(x.shape, x.dtype) for x in out] if away_out else out,
        in_specs=[pl.BlockSpec(memory_space=pltpu.SMEM)]
        + [pl.BlockSpec(memory_space=pltpu.HBM)] * fetched
        + [vmem] * (len(operands) - fetched),
        out_specs=[vmem] * len(shapes),
        scratch_shapes=list(scratch)
        + ([pltpu.VMEM(x.shape, x.dtype) for x in away] + [pltpu.SemaphoreType.DMA((fetched,))] if away else []),
        compiler_params=pltpu.CompilerParams(vmem_limit_bytes=LIMIT),
        cost_estimate=pl.CostEstimate(
            flops=int(flops),
            bytes_accessed=sum(x.dtype.itemsize * math.prod(x.shape) for x in [*out, *operands]),
            transcendentals=0,
        ),
    )(flag, *[pltpu.with_memory_space_constraint(x, pltpu.HBM) for x in away], *operands[fetched:])


LIMIT = 30 << 20


def rim_call(flag, own, other, gain, wk, wv):
    D, W = wk.shape
    T = 4 * own.shape[1]
    return call(
        rim_kernel, [(T // 2, W)] * 2 + [jax.ShapeDtypeStruct((T, D), BF16)] * 3,
        flag, [own, wk, wv, other, gain], flops=2 * T * D * W * 6,
    )


def still_call(scale, flag, parts, wq, wk, wv):
    D, W = wk.shape
    T, hd = parts[0].shape[0], W // 2
    return call(
        functools.partial(still_kernel, scale), [(T, hd)] * 2 + [(T, W), (T, T), (T, hd)],
        flag, [wk, wv, wq, *parts], scratch=[pltpu.VMEM((T, W), F32)], flops=2 * T * D * hd * 24 + 2 * T * T * hd * 9, away_out=True,
    )


def moved_call(scale, flag, q, first, last, low, high, out_still, wo):
    T, hd = out_still.shape
    D = wo.shape[1]
    return call(
        functools.partial(moved_kernel, scale), [(2, T // 2, T), (2, T // 4, D), (2, T // 4, D)],
        flag, [q, first, last, wo, out_still, low, high],
        scratch=[pltpu.VMEM((T, 2 * hd), F32)], flops=2 * T * D * hd * 6 + 2 * T * T * hd * 9, fetched=5,
    )


def moved_back_call(scale, flag, own, other, wo, q, first, last, low, high, pm):
    T, hd = q.shape
    D = wo.shape[1]
    return call(
        functools.partial(moved_back_kernel, scale),
        [(T, hd), (T, hd), (T // 2, 2 * hd), (T // 2, 2 * hd), (T, 2 * hd)],
        flag, [q, low, first, pm, last, high, own, other, wo],
        scratch=[pltpu.VMEM((T, D), BF16)] * 2 + [pltpu.VMEM((T, 2 * hd), F32)],
        flops=2 * T * D * hd * 6 + 2 * T * T * hd * 12, away_out=True,
    )


def still_back_call(scale, flag, ga, q, kv, ps, dqm, wq, wk, wv):
    T, hd = dqm.shape
    D = wq.shape[0]
    return call(
        functools.partial(still_back_kernel, scale), [(T, D)],
        flag, [ga, kv, ps, q, dqm, wq, wk, wv],
        scratch=[pltpu.VMEM((T, 2 * hd), F32)], flops=2 * T * D * hd * 12 + 2 * T * T * hd * 12, fetched=8,
    )[0]


def finish_call(flag, terms, keep, left, right, wk, wv):
    T, D = terms.shape
    return call(
        finish_kernel, [(2, T // 4, D)] * 2,
        flag, [wk, wv, terms, keep, left, right], flops=2 * T * D * wk.shape[1] * 3,
    )


CHIP = 2


def core_swap(x):
    length = lax.axis_size("head")
    return lax.ppermute(x, "head", [(i, i ^ 1) for i in range(length)])


def same_core():
    length = lax.axis_size("head")
    return [list(range(core, length, CHIP)) for core in range(CHIP)]


def gather_chips(rows):
    groups = same_core()
    chips = len(groups[0])
    sent = jnp.broadcast_to(rows[None], (chips,) + rows.shape)
    own = lax.all_to_all(sent, "head", 0, 0, tiled=True, axis_index_groups=groups)
    return own.reshape(2, -1, rows.shape[1])


def sum_chips(part):
    groups = same_core()
    chips = len(groups[0])
    split = part.reshape(chips, -1, part.shape[2])
    swapped = lax.all_to_all(split, "head", 0, 0, tiled=True, axis_index_groups=groups)
    return jnp.sum(swapped, axis=0)


def along(x, by):
    length = lax.axis_size("ctx")
    return lax.ppermute(x, "ctx", [(i, (i + by) % length) for i in range(length)])


def layer(tokens, norm_gain, w_query, w_key, w_value, w_out, shift_heads, cotangent):
    scale = 1.0 / math.sqrt(w_query.shape[1] // 2)
    flag = shift_heads[1:2]
    gain = norm_gain[None]
    own = gather_chips(tokens)
    own, cot_later = lax.optimization_barrier((own, cotangent))
    other = core_swap(own)
    cot_own = gather_chips(cot_later)
    first, last, *parts = rim_call(flag, own, other, gain, w_key, w_value)
    low, high = along(last, 1), along(first, -1)
    query_moved, query_still, kv_still, probs_still, out_still = still_call(scale, flag, parts, w_query, w_key, w_value)
    cot_own, out_still = lax.optimization_barrier((cot_own, out_still))
    cot_other = core_swap(cot_own)
    probs_moved, mine, theirs = moved_call(scale, flag, query_moved, first, last, low, high, out_still, w_out)
    out_part = mine + core_swap(theirs)
    grad_still, grad_query, left, right, keep = moved_back_call(
        scale, flag, cot_own, cot_other, w_out, query_moved, first, last, low, high, probs_moved
    )
    grad_query, out_part = lax.optimization_barrier((grad_query, out_part))
    out_sum = sum_chips(out_part)
    from_left, from_right = along(right, 1), along(left, -1)
    terms = still_back_call(
        scale, flag, grad_still, query_still, kv_still, probs_still, grad_query, w_query, w_key, w_value
    )
    mine, theirs = finish_call(flag, terms, keep, from_left, from_right, w_key, w_value)
    grad_part, out_sum = lax.optimization_barrier((mine + core_swap(theirs), out_sum))
    grad_sum = sum_chips(grad_part)
    mixed = tokens + out_sum
    inverse = lax.rsqrt(jnp.mean(tokens * tokens, axis=-1, keepdims=True) + 1e-06)
    weighted = grad_sum * norm_gain
    correction = jnp.mean(weighted * tokens, axis=-1, keepdims=True)
    input_grad = (
        cotangent + weighted * inverse - tokens * (inverse * inverse * inverse) * correction
    )
    return (mixed, input_grad)


def solution(mesh):
    placed = (
        P(("ctx", "head"), None),
        P(),
        P(None, "head"),
        P(None, "head"),
        P(None, "head"),
        P("head", None),
        P("head"),
        P(("ctx", "head"), None),
    )
    return jax.shard_map(
        layer,
        mesh=mesh,
        in_specs=placed,
        out_specs=(P(("ctx", "head"), None), P(("ctx", "head"), None)),
        check_vma=False,
    )
```

```python
import functools
import math

import jax
import jax.numpy as jnp
from jax import lax
from jax.experimental import pallas as pl
from jax.experimental.pallas import tpu as pltpu
from jax.sharding import PartitionSpec as P

F32, BF16 = jnp.float32, jnp.bfloat16
NN, NT, TN = ((1,), (0,)), ((1,), (1,)), ((0,), (0,))


def parts2(x):
    high = x.astype(BF16)
    return high, (x - high.astype(F32)).astype(BF16)


def parts3(x):
    high = x.astype(BF16)
    rest = x - high.astype(F32)
    middle = rest.astype(BF16)
    return high, middle, (rest - middle.astype(F32)).astype(BF16)


def mul(a, b, dims):
    return lax.dot_general(a, b, (dims, ((), ())), preferred_element_type=F32)


def mul3(a, b, dims):
    return mul(a[0], b[0], dims) + (mul(a[0], b[1], dims) + mul(a[1], b[0], dims))


def mul6(a, b, dims):
    small = mul(a[1], b[1], dims) + mul(a[0], b[2], dims) + mul(a[2], b[0], dims)
    return mul(a[0], b[0], dims) + (mul(a[0], b[1], dims) + mul(a[1], b[0], dims) + small)


def cat(a, b):
    return jnp.concatenate([a, b], axis=1)


def scores6(a, b):
    (ah, am, al), (bh, bm, bl) = a, b
    wide = cat(bh, bm)
    return mul(cat(ah, ah), wide, NT) + (mul(cat(am, am), wide, NT) + mul(cat(ah, al), cat(bl, bh), NT))


def scores3(a, b):
    (ah, am), (bh, bm) = a, b
    return mul(cat(ah, am), cat(bh, bh), NT) + mul(ah, bm, NT)


def weigh3(a, b, dims):
    width = b[0].shape[1]
    both = mul(a[0], cat(b[0], b[1]), dims)
    return both[:, :width] + (both[:, width:] + mul(a[1], b[0], dims))


def head_cols(flag_ref, width):
    second = flag_ref[0]
    moved = pl.multiple_of(second * width, width)
    still = pl.multiple_of((1 - second) * width, width)
    return pl.ds(moved, width), pl.ds(still, width)


def normed_parts(own, other, gain_ref, refs):
    for slot, source in ((1, other), (0, own)):
        rows = source.shape[1]
        if isinstance(source, Fetched):
            source = source.ready()

        @pl.loop(0, 2)
        def _(half):
            x = source[half]
            x = x * lax.rsqrt(jnp.mean(x * x, axis=-1, keepdims=True) + 1e-06) * gain_ref[...]
            at = pl.ds(pl.multiple_of((2 * half + slot) * rows, rows), rows)
            for ref, part in zip(refs, parts3(x)):
                ref[at] = part


def softmax_rows(scores):
    powers = jnp.exp(scores - jnp.max(scores, axis=-1, keepdims=True))
    return powers / jnp.sum(powers, axis=-1, keepdims=True)


def rim_kernel(flag_ref, own, wk, wv, other, gain_ref, first_ref, last_ref, nh, nm, nl):
    normed_parts(own, other, gain_ref, (nh, nm, nl))
    moved, _ = head_cols(flag_ref, wk.shape[1] // 2)
    half = first_ref.shape[0]
    both = mul6((nh[...], nm[...], nl[...]), parts3(cat(wk[:, moved], wv[:, moved])), NN)
    first_ref[...] = both[:half]
    last_ref[...] = both[half:]


def still_kernel(scale, flag_ref, wk, wv, wq, nh, nm, nl, qm_ref, qs_ref, kv_ref, ps_ref, os_ref, q_ref):
    hd = wk.shape[1] // 2
    moved, still = head_cols(flag_ref, hd)
    n = (nh[...], nm[...], nl[...])
    kv_ref[...] = mul6(n, parts3(cat(wk[:, still], wv[:, still])), NN)
    q_ref[...] = mul6(n, parts3(wq[...]), NN)
    qm_ref[...] = q_ref[:, moved]
    qs_ref[...] = q_ref[:, still]
    scores = scores6(parts3(qs_ref[...]), parts3(kv_ref[:, :hd])) * scale
    probs = softmax_rows(scores)
    ps_ref[...] = probs
    os_ref[...] = weigh3(parts2(probs), parts2(kv_ref[:, hd:]), NN)


def moved_kernel(scale, flag_ref, q_ref, first_ref, last_ref, wo, os_ref, low_ref, high_ref, pm_ref, mine_ref, theirs_ref, both):
    hd = os_ref.shape[1]
    half = first_ref.shape[0]
    moved, still = head_cols(flag_ref, hd)
    for g, (a_ref, b_ref) in enumerate(((low_ref, first_ref), (last_ref, high_ref))):
        rim = jnp.concatenate([a_ref[...], b_ref[...]], axis=0)
        at = pl.ds(g * half, half)
        scores = scores6(parts3(q_ref[at]), parts3(rim[:, :hd])) * scale
        probs = softmax_rows(scores)
        pm_ref[g] = probs
        both[at, moved] = weigh3(parts2(probs), parts2(rim[:, hd:]), NN)
    both[:, still] = os_ref[...]
    rows = mine_ref.shape[1]
    out = mul3(parts2(both[...]), parts2(wo[...]), NN)
    for g in range(2):
        mine_ref[g] = out[2 * g * rows : (2 * g + 1) * rows]
        theirs_ref[g] = out[(2 * g + 1) * rows : (2 * g + 2) * rows]


def group_back(query, kv, probs, grad_out, scale):
    hd = query.shape[1]
    q, k, v, g = parts2(query), parts2(kv[:, :hd]), parts2(kv[:, hd:]), parts2(grad_out)
    grad_probs = scores3(g, v)
    inner = jnp.sum(probs * grad_probs, axis=-1, keepdims=True)
    grad_values = weigh3(parts2(probs), g, TN)
    grad_scores = parts2(probs * (grad_probs - inner) * scale)
    grad_query = weigh3(grad_scores, k, NN)
    grad_keys = weigh3(grad_scores, q, TN)
    return grad_query, cat(grad_keys, grad_values)


def moved_back_kernel(scale, flag_ref, q, rim_low, rim_first, pm, rim_last, rim_high, own, other, wo, gs_ref, dq_ref, left_ref, right_ref, keep_ref, ch, cm, ga_ref):
    for slot, source in enumerate((own, other)):
        rows = source.shape[1]
        for g in range(2):
            at = pl.ds((2 * g + slot) * rows, rows)
            ch[at], cm[at] = parts2(source[g])
    moved, still = head_cols(flag_ref, q.shape[1])
    ga_ref[...] = mul3((ch[...], cm[...]), parts2(wo[...]), NT)
    gs_ref[...] = ga_ref[:, still]
    for g, (a, b) in enumerate(((rim_low, rim_first), (rim_last, rim_high))):
        rim = jnp.concatenate([a[...], b[...]], axis=0)
        half = left_ref.shape[0]
        at = pl.ds(g * half, half)
        gq, gkv = group_back(q[at], rim, pm[g], ga_ref[at, moved], scale)
        dq_ref[at] = gq
        if g == 0:
            left_ref[...] = gkv[:half]
            keep_ref[:half] = gkv[half:]
        else:
            keep_ref[half:] = gkv[:half]
            right_ref[...] = gkv[half:]


def still_back_kernel(scale, flag_ref, ga, kv, ps, q, dqm, wq, wk, wv, terms_ref, both):
    hd = dqm.shape[1]
    moved, still = head_cols(flag_ref, hd)
    gq, gkv = group_back(q[...], kv[...], ps[...], ga[...], scale)
    both[:, moved] = dqm[...]
    both[:, still] = gq
    terms_ref[...] = mul3(parts2(both[...]), parts2(wq[...]), NT)
    terms_ref[...] += mul3(parts2(gkv), parts2(cat(wk[:, still], wv[:, still])), NT)


def finish_kernel(flag_ref, wk, wv, terms_ref, keep_ref, left_ref, right_ref, mine_ref, theirs_ref):
    moved, _ = head_cols(flag_ref, wk.shape[1] // 2)
    rows = mine_ref.shape[1]
    grads = keep_ref[...] + jnp.concatenate([left_ref[...], right_ref[...]], axis=0)
    out = terms_ref[...] + mul3(parts2(grads), parts2(cat(wk[:, moved], wv[:, moved])), NT)
    for h in range(2):
        mine_ref[h] = out[2 * h * rows : (2 * h + 1) * rows]
        theirs_ref[h] = out[(2 * h + 1) * rows : (2 * h + 2) * rows]


class Fetched:
    def __init__(self, source, held, semaphore):
        self.copy, self.held, self.waiting = pltpu.make_async_copy(source, held, semaphore), held, True
        self.copy.start()

    @property
    def shape(self):
        return self.held.shape

    def ready(self):
        if self.waiting:
            self.copy.wait()
            self.waiting = False
        return self.held

    def __getitem__(self, at):
        return self.ready()[at]


def call(kernel, shapes, flag, operands, scratch=(), flops=0, fetched=0, away_out=False):
    vmem = pl.BlockSpec(memory_space=pltpu.VMEM)
    out = [s if isinstance(s, jax.ShapeDtypeStruct) else jax.ShapeDtypeStruct(s, F32) for s in shapes]
    away = operands[:fetched]

    def body(flag_ref, *refs):
        if away:
            sources, rest, held, semaphores = refs[:fetched], refs[fetched : -1 - fetched], refs[-1 - fetched : -1], refs[-1]
            refs = [Fetched(x, h, semaphores.at[i]) for i, (x, h) in enumerate(zip(sources, held))] + list(rest)
        kernel(flag_ref, *refs)

    return pl.pallas_call(
        body,
        out_shape=[pltpu.HBM(x.shape, x.dtype) for x in out] if away_out else out,
        in_specs=[pl.BlockSpec(memory_space=pltpu.SMEM)]
        + [pl.BlockSpec(memory_space=pltpu.HBM)] * fetched
        + [vmem] * (len(operands) - fetched),
        out_specs=[vmem] * len(shapes),
        scratch_shapes=list(scratch)
        + ([pltpu.VMEM(x.shape, x.dtype) for x in away] + [pltpu.SemaphoreType.DMA((fetched,))] if away else []),
        compiler_params=pltpu.CompilerParams(vmem_limit_bytes=LIMIT),
        cost_estimate=pl.CostEstimate(
            flops=int(flops),
            bytes_accessed=sum(x.dtype.itemsize * math.prod(x.shape) for x in [*out, *operands]),
            transcendentals=0,
        ),
    )(flag, *[pltpu.with_memory_space_constraint(x, pltpu.HBM) for x in away], *operands[fetched:])


LIMIT = 30 << 20


def rim_call(flag, own, other, gain, wk, wv):
    D, W = wk.shape
    T = 4 * own.shape[1]
    return call(
        rim_kernel, [(T // 2, W)] * 2 + [jax.ShapeDtypeStruct((T, D), BF16)] * 3,
        flag, [own, wk, wv, other, gain], flops=2 * T * D * W * 6, fetched=3,
    )


def still_call(scale, flag, parts, wq, wk, wv):
    D, W = wk.shape
    T, hd = parts[0].shape[0], W // 2
    return call(
        functools.partial(still_kernel, scale), [(T, hd)] * 2 + [(T, W), (T, T), (T, hd)],
        flag, [wk, wv, wq, *parts], scratch=[pltpu.VMEM((T, W), F32)], flops=2 * T * D * hd * 24 + 2 * T * T * hd * 9, away_out=True,
    )


def moved_call(scale, flag, q, first, last, low, high, out_still, wo):
    T, hd = out_still.shape
    D = wo.shape[1]
    return call(
        functools.partial(moved_kernel, scale), [(2, T // 2, T), (2, T // 4, D), (2, T // 4, D)],
        flag, [q, first, last, wo, out_still, low, high],
        scratch=[pltpu.VMEM((T, 2 * hd), F32)], flops=2 * T * D * hd * 6 + 2 * T * T * hd * 9, fetched=5,
    )


def moved_back_call(scale, flag, own, other, wo, q, first, last, low, high, pm):
    T, hd = q.shape
    D = wo.shape[1]
    return call(
        functools.partial(moved_back_kernel, scale),
        [(T, hd), (T, hd), (T // 2, 2 * hd), (T // 2, 2 * hd), (T, 2 * hd)],
        flag, [q, low, first, pm, last, high, own, other, wo],
        scratch=[pltpu.VMEM((T, D), BF16)] * 2 + [pltpu.VMEM((T, 2 * hd), F32)],
        flops=2 * T * D * hd * 6 + 2 * T * T * hd * 12, away_out=True,
    )


def still_back_call(scale, flag, ga, q, kv, ps, dqm, wq, wk, wv):
    T, hd = dqm.shape
    D = wq.shape[0]
    return call(
        functools.partial(still_back_kernel, scale), [(T, D)],
        flag, [ga, kv, ps, q, dqm, wq, wk, wv],
        scratch=[pltpu.VMEM((T, 2 * hd), F32)], flops=2 * T * D * hd * 12 + 2 * T * T * hd * 12, fetched=8,
    )[0]


def finish_call(flag, terms, keep, left, right, wk, wv):
    T, D = terms.shape
    return call(
        finish_kernel, [(2, T // 4, D)] * 2,
        flag, [wk, wv, terms, keep, left, right], flops=2 * T * D * wk.shape[1] * 3,
    )


CHIP = 2


def core_swap(x):
    length = lax.axis_size("head")
    return lax.ppermute(x, "head", [(i, i ^ 1) for i in range(length)])


def same_core():
    length = lax.axis_size("head")
    return [list(range(core, length, CHIP)) for core in range(CHIP)]


def gather_chips(rows):
    groups = same_core()
    chips = len(groups[0])
    sent = jnp.broadcast_to(rows[None], (chips,) + rows.shape)
    own = lax.all_to_all(sent, "head", 0, 0, tiled=True, axis_index_groups=groups)
    return own.reshape(2, -1, rows.shape[1])


def sum_chips(part):
    groups = same_core()
    chips = len(groups[0])
    split = part.reshape(chips, -1, part.shape[2])
    swapped = lax.all_to_all(split, "head", 0, 0, tiled=True, axis_index_groups=groups)
    return jnp.sum(swapped, axis=0)


def along(x, by):
    length = lax.axis_size("ctx")
    return lax.ppermute(x, "ctx", [(i, (i + by) % length) for i in range(length)])


def layer(tokens, norm_gain, w_query, w_key, w_value, w_out, shift_heads, cotangent):
    scale = 1.0 / math.sqrt(w_query.shape[1] // 2)
    flag = shift_heads[1:2]
    gain = norm_gain[None]
    own = gather_chips(tokens)
    own, cot_later = lax.optimization_barrier((own, cotangent))
    other = core_swap(own)
    cot_own = gather_chips(cot_later)
    first, last, *parts = rim_call(flag, own, other, gain, w_key, w_value)
    low, high = along(last, 1), along(first, -1)
    query_moved, query_still, kv_still, probs_still, out_still = still_call(scale, flag, parts, w_query, w_key, w_value)
    cot_own, out_still = lax.optimization_barrier((cot_own, out_still))
    cot_other = core_swap(cot_own)
    probs_moved, mine, theirs = moved_call(scale, flag, query_moved, first, last, low, high, out_still, w_out)
    out_part = mine + core_swap(theirs)
    grad_still, grad_query, left, right, keep = moved_back_call(
        scale, flag, cot_own, cot_other, w_out, query_moved, first, last, low, high, probs_moved
    )
    grad_query, out_part = lax.optimization_barrier((grad_query, out_part))
    out_sum = sum_chips(out_part)
    from_left, from_right = along(right, 1), along(left, -1)
    terms = still_back_call(
        scale, flag, grad_still, query_still, kv_still, probs_still, grad_query, w_query, w_key, w_value
    )
    mine, theirs = finish_call(flag, terms, keep, from_left, from_right, w_key, w_value)
    grad_part, out_sum = lax.optimization_barrier((mine + core_swap(theirs), out_sum))
    grad_sum = sum_chips(grad_part)
    mixed = tokens + out_sum
    inverse = lax.rsqrt(jnp.mean(tokens * tokens, axis=-1, keepdims=True) + 1e-06)
    weighted = grad_sum * norm_gain
    correction = jnp.mean(weighted * tokens, axis=-1, keepdims=True)
    input_grad = (
        cotangent + weighted * inverse - tokens * (inverse * inverse * inverse) * correction
    )
    return (mixed, input_grad)


def solution(mesh):
    placed = (
        P(("ctx", "head"), None),
        P(),
        P(None, "head"),
        P(None, "head"),
        P(None, "head"),
        P("head", None),
        P("head"),
        P(("ctx", "head"), None),
    )
    return jax.shard_map(
        layer,
        mesh=mesh,
        in_specs=placed,
        out_specs=(P(("ctx", "head"), None), P(("ctx", "head"), None)),
        check_vma=False,
    )
```

```python
import functools
import math

import jax
import jax.numpy as jnp
from jax import lax
from jax.experimental import pallas as pl
from jax.experimental.pallas import tpu as pltpu
from jax.sharding import PartitionSpec as P

F32, BF16 = jnp.float32, jnp.bfloat16
NN, NT, TN = ((1,), (0,)), ((1,), (1,)), ((0,), (0,))


def parts2(x):
    high = x.astype(BF16)
    return high, (x - high.astype(F32)).astype(BF16)


def parts3(x):
    high = x.astype(BF16)
    rest = x - high.astype(F32)
    middle = rest.astype(BF16)
    return high, middle, (rest - middle.astype(F32)).astype(BF16)


def mul(a, b, dims):
    return lax.dot_general(a, b, (dims, ((), ())), preferred_element_type=F32)


def mul3(a, b, dims):
    return mul(a[0], b[0], dims) + (mul(a[0], b[1], dims) + mul(a[1], b[0], dims))


def mul6(a, b, dims):
    small = mul(a[1], b[1], dims) + mul(a[0], b[2], dims) + mul(a[2], b[0], dims)
    return mul(a[0], b[0], dims) + (mul(a[0], b[1], dims) + mul(a[1], b[0], dims) + small)


def cat(a, b):
    return jnp.concatenate([a, b], axis=1)


def scores6(a, b):
    (ah, am, al), (bh, bm, bl) = a, b
    wide = cat(bh, bm)
    return mul(cat(ah, ah), wide, NT) + (mul(cat(am, am), wide, NT) + mul(cat(ah, al), cat(bl, bh), NT))


def scores3(a, b):
    (ah, am), (bh, bm) = a, b
    return mul(cat(ah, am), cat(bh, bh), NT) + mul(ah, bm, NT)


def weigh3(a, b, dims):
    width = b[0].shape[1]
    both = mul(a[0], cat(b[0], b[1]), dims)
    return both[:, :width] + (both[:, width:] + mul(a[1], b[0], dims))


def head_cols(flag_ref, width):
    second = flag_ref[0]
    moved = pl.multiple_of(second * width, width)
    still = pl.multiple_of((1 - second) * width, width)
    return pl.ds(moved, width), pl.ds(still, width)


def normed_parts(own, other, gain_ref, refs):
    for slot, source in ((1, other), (0, own)):
        rows = source.shape[1]
        if isinstance(source, Fetched):
            source = source.ready()

        @pl.loop(0, 2)
        def _(half):
            x = source[half]
            x = x * lax.rsqrt(jnp.mean(x * x, axis=-1, keepdims=True) + 1e-06) * gain_ref[...]
            at = pl.ds(pl.multiple_of((2 * half + slot) * rows, rows), rows)
            for ref, part in zip(refs, parts3(x)):
                ref[at] = part


def softmax_rows(scores):
    powers = jnp.exp(scores - jnp.max(scores, axis=-1, keepdims=True))
    return powers / jnp.sum(powers, axis=-1, keepdims=True)


def rim_kernel(flag_ref, own, wk, wv, other, gain_ref, first_ref, last_ref, nh, nm, nl):
    normed_parts(own, other, gain_ref, (nh, nm, nl))
    moved, _ = head_cols(flag_ref, wk.shape[1] // 2)
    half = first_ref.shape[0]
    both = mul6((nh[...], nm[...], nl[...]), parts3(cat(wk[:, moved], wv[:, moved])), NN)
    first_ref[...] = both[:half]
    last_ref[...] = both[half:]


def still_kernel(scale, flag_ref, wk, wv, wq, nh, nm, nl, qm_ref, qs_ref, kv_ref, ps_ref, os_ref, q_ref):
    hd = wk.shape[1] // 2
    moved, still = head_cols(flag_ref, hd)
    n = (nh[...], nm[...], nl[...])
    kv_ref[...] = mul6(n, parts3(cat(wk[:, still], wv[:, still])), NN)
    q_ref[...] = mul6(n, parts3(wq[...]), NN)
    qm_ref[...] = q_ref[:, moved]
    qs_ref[...] = q_ref[:, still]
    scores = scores6(parts3(qs_ref[...]), parts3(kv_ref[:, :hd])) * scale
    probs = softmax_rows(scores)
    ps_ref[...] = probs
    os_ref[...] = weigh3(parts2(probs), parts2(kv_ref[:, hd:]), NN)


def moved_kernel(scale, flag_ref, q_ref, first_ref, last_ref, wo, os_ref, low_ref, high_ref, pm_ref, mine_ref, theirs_ref, both):
    hd = os_ref.shape[1]
    half = first_ref.shape[0]
    moved, still = head_cols(flag_ref, hd)
    for g, (a_ref, b_ref) in enumerate(((low_ref, first_ref), (last_ref, high_ref))):
        rim = jnp.concatenate([a_ref[...], b_ref[...]], axis=0)
        at = pl.ds(g * half, half)
        scores = scores6(parts3(q_ref[at]), parts3(rim[:, :hd])) * scale
        probs = softmax_rows(scores)
        pm_ref[g] = probs
        both[at, moved] = weigh3(parts2(probs), parts2(rim[:, hd:]), NN)
    both[:, still] = os_ref[...]
    rows = mine_ref.shape[1]
    out = mul3(parts2(both[...]), parts2(wo[...]), NN)
    for g in range(2):
        mine_ref[g] = out[2 * g * rows : (2 * g + 1) * rows]
        theirs_ref[g] = out[(2 * g + 1) * rows : (2 * g + 2) * rows]


def group_back(query, kv, probs, grad_out, scale):
    hd = query.shape[1]
    q, k, v, g = parts2(query), parts2(kv[:, :hd]), parts2(kv[:, hd:]), parts2(grad_out)
    grad_probs = scores3(g, v)
    inner = jnp.sum(probs * grad_probs, axis=-1, keepdims=True)
    grad_values = weigh3(parts2(probs), g, TN)
    grad_scores = parts2(probs * (grad_probs - inner) * scale)
    grad_query = weigh3(grad_scores, k, NN)
    grad_keys = weigh3(grad_scores, q, TN)
    return grad_query, cat(grad_keys, grad_values)


def moved_back_kernel(scale, flag_ref, q, rim_low, rim_first, pm, rim_last, rim_high, own, other, wo, gs_ref, dq_ref, left_ref, right_ref, keep_ref, ch, cm, ga_ref):
    for slot, source in enumerate((own, other)):
        rows = source.shape[1]
        for g in range(2):
            at = pl.ds((2 * g + slot) * rows, rows)
            ch[at], cm[at] = parts2(source[g])
    moved, still = head_cols(flag_ref, q.shape[1])
    ga_ref[...] = mul3((ch[...], cm[...]), parts2(wo[...]), NT)
    gs_ref[...] = ga_ref[:, still]
    for g, (a, b) in enumerate(((rim_low, rim_first), (rim_last, rim_high))):
        rim = jnp.concatenate([a[...], b[...]], axis=0)
        half = left_ref.shape[0]
        at = pl.ds(g * half, half)
        gq, gkv = group_back(q[at], rim, pm[g], ga_ref[at, moved], scale)
        dq_ref[at] = gq
        if g == 0:
            left_ref[...] = gkv[:half]
            keep_ref[:half] = gkv[half:]
        else:
            keep_ref[half:] = gkv[:half]
            right_ref[...] = gkv[half:]


def still_back_kernel(scale, flag_ref, ga, kv, ps, q, dqm, wq, wk, wv, terms_ref, both):
    hd = dqm.shape[1]
    moved, still = head_cols(flag_ref, hd)
    gq, gkv = group_back(q[...], kv[...], ps[...], ga[...], scale)
    both[:, moved] = dqm[...]
    both[:, still] = gq
    terms_ref[...] = mul3(parts2(both[...]), parts2(wq[...]), NT)
    terms_ref[...] += mul3(parts2(gkv), parts2(cat(wk[:, still], wv[:, still])), NT)


def finish_kernel(flag_ref, wk, wv, terms_ref, keep_ref, left_ref, right_ref, mine_ref, theirs_ref):
    moved, _ = head_cols(flag_ref, wk.shape[1] // 2)
    rows = mine_ref.shape[1]
    grads = keep_ref[...] + jnp.concatenate([left_ref[...], right_ref[...]], axis=0)
    out = terms_ref[...] + mul3(parts2(grads), parts2(cat(wk[:, moved], wv[:, moved])), NT)
    for h in range(2):
        mine_ref[h] = out[2 * h * rows : (2 * h + 1) * rows]
        theirs_ref[h] = out[(2 * h + 1) * rows : (2 * h + 2) * rows]


class Fetched:
    def __init__(self, source, held, semaphore):
        self.copy, self.held, self.waiting = pltpu.make_async_copy(source, held, semaphore), held, True
        self.copy.start()

    @property
    def shape(self):
        return self.held.shape

    def ready(self):
        if self.waiting:
            self.copy.wait()
            self.waiting = False
        return self.held

    def __getitem__(self, at):
        return self.ready()[at]


def call(kernel, shapes, flag, operands, scratch=(), flops=0, fetched=0, away_out=False):
    vmem = pl.BlockSpec(memory_space=pltpu.VMEM)
    out = [s if isinstance(s, jax.ShapeDtypeStruct) else jax.ShapeDtypeStruct(s, F32) for s in shapes]
    away = operands[:fetched]

    def body(flag_ref, *refs):
        if away:
            sources, rest, held, semaphores = refs[:fetched], refs[fetched : -1 - fetched], refs[-1 - fetched : -1], refs[-1]
            refs = [Fetched(x, h, semaphores.at[i]) for i, (x, h) in enumerate(zip(sources, held))] + list(rest)
        kernel(flag_ref, *refs)

    return pl.pallas_call(
        body,
        out_shape=[pltpu.HBM(x.shape, x.dtype) for x in out] if away_out else out,
        in_specs=[pl.BlockSpec(memory_space=pltpu.SMEM)]
        + [pl.BlockSpec(memory_space=pltpu.HBM)] * fetched
        + [vmem] * (len(operands) - fetched),
        out_specs=[vmem] * len(shapes),
        scratch_shapes=list(scratch)
        + ([pltpu.VMEM(x.shape, x.dtype) for x in away] + [pltpu.SemaphoreType.DMA((fetched,))] if away else []),
        compiler_params=pltpu.CompilerParams(vmem_limit_bytes=LIMIT),
        cost_estimate=pl.CostEstimate(
            flops=int(flops),
            bytes_accessed=sum(x.dtype.itemsize * math.prod(x.shape) for x in [*out, *operands]),
            transcendentals=0,
        ),
    )(flag, *[pltpu.with_memory_space_constraint(x, pltpu.HBM) for x in away], *operands[fetched:])


LIMIT = 30 << 20


def rim_call(flag, own, other, gain, wk, wv):
    D, W = wk.shape
    T = 4 * own.shape[1]
    return call(
        rim_kernel, [(T // 2, W)] * 2 + [jax.ShapeDtypeStruct((T, D), BF16)] * 3,
        flag, [own, wk, wv, other, gain], flops=2 * T * D * W * 6, fetched=3,
    )


def still_call(scale, flag, parts, wq, wk, wv):
    D, W = wk.shape
    T, hd = parts[0].shape[0], W // 2
    return call(
        functools.partial(still_kernel, scale), [(T, hd)] * 2 + [(T, W), (T, T), (T, hd)],
        flag, [wk, wv, wq, *parts], scratch=[pltpu.VMEM((T, W), F32)], flops=2 * T * D * hd * 24 + 2 * T * T * hd * 9, away_out=True,
    )


def moved_call(scale, flag, q, first, last, low, high, out_still, wo):
    T, hd = out_still.shape
    D = wo.shape[1]
    return call(
        functools.partial(moved_kernel, scale), [(2, T // 2, T), (2, T // 4, D), (2, T // 4, D)],
        flag, [q, first, last, wo, out_still, low, high],
        scratch=[pltpu.VMEM((T, 2 * hd), F32)], flops=2 * T * D * hd * 6 + 2 * T * T * hd * 9, fetched=5,
    )


def moved_back_call(scale, flag, own, other, wo, q, first, last, low, high, pm):
    T, hd = q.shape
    D = wo.shape[1]
    return call(
        functools.partial(moved_back_kernel, scale),
        [(T, hd), (T, hd), (T // 2, 2 * hd), (T // 2, 2 * hd), (T, 2 * hd)],
        flag, [q, low, first, pm, last, high, own, other, wo],
        scratch=[pltpu.VMEM((T, D), BF16)] * 2 + [pltpu.VMEM((T, 2 * hd), F32)],
        flops=2 * T * D * hd * 6 + 2 * T * T * hd * 12, away_out=True,
    )


def still_back_call(scale, flag, ga, q, kv, ps, dqm, wq, wk, wv):
    T, hd = dqm.shape
    D = wq.shape[0]
    return call(
        functools.partial(still_back_kernel, scale), [(T, D)],
        flag, [ga, kv, ps, q, dqm, wq, wk, wv],
        scratch=[pltpu.VMEM((T, 2 * hd), F32)], flops=2 * T * D * hd * 12 + 2 * T * T * hd * 12, fetched=8,
    )[0]


def finish_call(flag, terms, keep, left, right, wk, wv):
    T, D = terms.shape
    return call(
        finish_kernel, [(2, T // 4, D)] * 2,
        flag, [wk, wv, terms, keep, left, right], flops=2 * T * D * wk.shape[1] * 3,
    )


def halves_kernel(flag_ref, mine_ref, other_ref, kept_ref, given_ref):
    place = lax.axis_index("head") // 2 % 2
    kept_ref[...] = mine_ref[:, place] + other_ref[:, place]
    given_ref[...] = mine_ref[:, 1 - place] + other_ref[:, 1 - place]


def halves_call(flag, mine, other):
    lines, _, rows, width = mine.shape
    return call(halves_kernel, [(lines, rows, width)] * 2, flag, [mine, other], flops=mine.size)


CHIP = 2
PAIR = 2


def core_swap(x):
    length = lax.axis_size("head")
    return lax.ppermute(x, "head", [(i, i ^ 1) for i in range(length)])


def same_core():
    length = lax.axis_size("head")
    return [list(range(core, length, CHIP)) for core in range(CHIP)]


def gather_chips(rows):
    groups = same_core()
    chips = len(groups[0])
    sent = jnp.broadcast_to(rows[None], (chips,) + rows.shape)
    own = lax.all_to_all(sent, "head", 0, 0, tiled=True, axis_index_groups=groups)
    return own.reshape(2, -1, rows.shape[1])


def sum_chips(part):
    groups = same_core()
    chips = len(groups[0])
    split = part.reshape(chips, -1, part.shape[2])
    swapped = lax.all_to_all(split, "head", 0, 0, tiled=True, axis_index_groups=groups)
    return jnp.sum(swapped, axis=0)


def pair_swap(x):
    length = lax.axis_size("head")
    return lax.ppermute(x, "head", [(i, i ^ CHIP) for i in range(length)])


def sum_line(part):
    length, step = lax.axis_size("head"), CHIP * PAIR
    groups = [list(range(place, length, step)) for place in range(step)]
    swapped = lax.all_to_all(part, "head", 0, 0, tiled=True, axis_index_groups=groups)
    return jnp.sum(swapped, axis=0)


def along(x, by):
    length = lax.axis_size("ctx")
    return lax.ppermute(x, "ctx", [(i, (i + by) % length) for i in range(length)])


def layer(tokens, norm_gain, w_query, w_key, w_value, w_out, shift_heads, cotangent):
    scale = 1.0 / math.sqrt(w_query.shape[1] // 2)
    flag = shift_heads[1:2]
    gain = norm_gain[None]
    own = gather_chips(tokens)
    own, cot_later = lax.optimization_barrier((own, cotangent))
    other = core_swap(own)
    cot_own = gather_chips(cot_later)
    first, last, *parts = rim_call(flag, own, other, gain, w_key, w_value)
    low, high = along(last, 1), along(first, -1)
    query_moved, query_still, kv_still, probs_still, out_still = still_call(scale, flag, parts, w_query, w_key, w_value)
    cot_own, out_still = lax.optimization_barrier((cot_own, out_still))
    out_still, cot_other = lax.optimization_barrier((out_still, core_swap(cot_own)))
    probs_moved, mine, theirs = moved_call(scale, flag, query_moved, first, last, low, high, out_still, w_out)
    lines = (lax.axis_size("head") // (CHIP * PAIR), PAIR, -1, tokens.shape[1])
    kept, given = halves_call(flag, mine.reshape(lines), core_swap(theirs).reshape(lines))
    received = pair_swap(given)
    grad_still, grad_query, left, right, keep = moved_back_call(
        scale, flag, cot_own, cot_other, w_out, query_moved, first, last, low, high, probs_moved
    )
    out_part = kept + received
    grad_query, out_part = lax.optimization_barrier((grad_query, out_part))
    out_sum = sum_line(out_part)
    from_left, from_right = along(right, 1), along(left, -1)
    terms = still_back_call(
        scale, flag, grad_still, query_still, kv_still, probs_still, grad_query, w_query, w_key, w_value
    )
    mine, theirs = finish_call(flag, terms, keep, from_left, from_right, w_key, w_value)
    grad_part, out_sum = lax.optimization_barrier((mine + core_swap(theirs), out_sum))
    grad_sum = sum_chips(grad_part)
    mixed = tokens + out_sum
    inverse = lax.rsqrt(jnp.mean(tokens * tokens, axis=-1, keepdims=True) + 1e-06)
    weighted = grad_sum * norm_gain
    correction = jnp.mean(weighted * tokens, axis=-1, keepdims=True)
    input_grad = (
        cotangent + weighted * inverse - tokens * (inverse * inverse * inverse) * correction
    )
    return (mixed, input_grad)


def solution(mesh):
    placed = (
        P(("ctx", "head"), None),
        P(),
        P(None, "head"),
        P(None, "head"),
        P(None, "head"),
        P("head", None),
        P("head"),
        P(("ctx", "head"), None),
    )
    return jax.shard_map(
        layer,
        mesh=mesh,
        in_specs=placed,
        out_specs=(P(("ctx", "head"), None), P(("ctx", "head"), None)),
        check_vma=False,
    )
```
